128 devices in a mesh: ctl: 8 (over z, y_hi), seq: 16 (over y_lo, x, core).
Axes of the slice: x: 4, y: 4 (y_hi: 2, y_lo: 2; y = y_hi * 2 + y_lo), z: 4, core: 2. Of those that a mesh axis runs over, the one named last changes fastest.
Arguments:
- control_hidden_state: bfloat16 [16, 64, 48, 3072], P('seq', None, 'ctl'), may hold values from -60 to 60
- patch_segment_labels: int32 [16, 64, 48], P('seq', None, 'ctl'), may hold values from 0 to 149
- patch_depth_levels: int32 [16, 64, 48], P('seq', None, 'ctl'), may hold values from 0 to 255
- timestep: int32 [16], replicated, may hold values from 0 to 999
- segment_label_embedding: bfloat16 [150, 3072], replicated, may hold values from -3 to 3
- depth_level_embedding: bfloat16 [256, 3072], replicated, may hold values from -3 to 3
- timestep_weight: bfloat16 [256, 3072], replicated, may hold values from -0.875 to 0.875
- control_norm_gain: float32 [3072], replicated, may hold values from 0.1 to 1.9
- control_output_weight: bfloat16 [3072, 3072], P('ctl'), may hold values from -0.109375 to 0.109375
- transformer_hidden_state: bfloat16 [16, 64, 48, 3072], P('ctl', 'seq'), may hold values from -3 to 3
- query: bfloat16 [16, 64, 48, 2048], P('ctl', 'seq'), may hold values from -5 to 5
- key: bfloat16 [16, 64, 48, 2048], P('ctl', 'seq'), may hold values from -5 to 5
- value: bfloat16 [16, 64, 48, 2048], P('ctl', 'seq'), may hold values from -12 to 12
- attention_output_weight: bfloat16 [2048, 3072], P('ctl'), may hold values from -0.125 to 0.125
Outputs:
- next_hidden: bfloat16 [16, 64, 48, 3072], P('ctl', 'seq')
The draws below stay inside these ranges and needn't reach their ends.
All inputs are finite; a program needn't handle non-finite values.
Results may differ from the reference program's by a relative error of at most 0.0059.
Values may be sent and summed in bfloat16 or wider, within the bound.
No kernel may reach another device: no remote copies, remote signals or barrier semaphores. Data moves between devices by JAX's collectives and lax.ppermute only.
A program may use at most 192 MiB of HBM per device.

```python
import math
import jax
import jax.numpy as jnp
from jax import lax

MODEL_WIDTH = 3072
HEADS = 16
HEAD_DIM = 128
SEG_CLASSES = 150
DEPTH_LEVELS = 256
FREQS = 256
STEPS_T = 1000
PATCH_ROWS = 64
PATCH_COLUMNS = 48
IMAGE_BATCH = 16
TOKENS = 3072
INNER = 2048


def drawn(key):
    base = jax.random.fold_in(key, 17)
    key_query, key_keys = jax.random.split(base, 2)
    array_shape = (IMAGE_BATCH, TOKENS, HEADS, HEAD_DIM)
    query_rows = jnp.clip(2.0 * jax.random.normal(key_query, array_shape, jnp.float32), -5.0, 5.0)
    keys_out = jnp.clip(jax.random.normal(key_keys, array_shape, jnp.float32), -5.0, 5.0)
    out_shape = (IMAGE_BATCH, PATCH_ROWS, PATCH_COLUMNS, HEADS * HEAD_DIM)
    return (query_rows.reshape(out_shape).astype(jnp.bfloat16), keys_out.reshape(out_shape).astype(jnp.bfloat16))


def draw_query(key, part):
    return drawn(key)[0]


def draw_key(key, part):
    return drawn(key)[1]


def draw_control_hidden_state(key, part):
    array_shape = (IMAGE_BATCH, PATCH_ROWS, PATCH_COLUMNS, MODEL_WIDTH)
    return jax.random.normal(key, array_shape, jnp.float32).astype(jnp.bfloat16)


def place_ends(result, rng, least, top_value):
    extent = result.shape
    spot = [jax.random.randint(jax.random.fold_in(rng, axis), (), 0, extent[axis]) for axis in range(len(extent))]
    result = result.at[tuple(spot)].set(least)
    longest = extent.index(max(extent))
    spot[longest] = (spot[longest] + 1) % extent[longest]
    return result.at[tuple(spot)].set(top_value)


def block_scale(rng, dims, cuts, least, top_value):
    def one(axis_at, shards_of):
        steps = jax.random.uniform(jax.random.fold_in(jax.random.fold_in(rng, 6), axis_at), (shards_of,), jnp.float32, least / len(cuts), top_value / len(cuts))
        return jnp.repeat(jnp.exp(steps), dims[axis_at] // shards_of).reshape((-1,) + (1,) * (len(dims) - axis_at - 1))

    level = one(*cuts[0])
    for cut in cuts[1:]:
        level = level * one(*cut)
    return level


def bell_draw(rng, extent, scale, bound, shards=(), held_as=jnp.bfloat16):
    drawn = scale * jax.random.normal(rng, extent, jnp.float32)
    if shards:
        drawn = drawn * block_scale(rng, extent, shards, -0.22, 0.18)
    return jnp.clip(drawn, -bound, bound).astype(held_as)


def setup_inputs(seed: int = 0) -> dict:
    key_list = jax.random.split(jax.random.key(seed), 15)
    return {
        "control_hidden_state": draw_control_hidden_state(jax.random.fold_in(key_list[14], 71), 0),
        "patch_segment_labels": place_ends(jax.random.randint(key_list[1], (IMAGE_BATCH, PATCH_ROWS, PATCH_COLUMNS), 0, SEG_CLASSES), jax.random.fold_in(key_list[1], 1), 0, SEG_CLASSES - 1).astype(jnp.int32),
        "patch_depth_levels": place_ends(jax.random.randint(key_list[2], (IMAGE_BATCH, PATCH_ROWS, PATCH_COLUMNS), 0, DEPTH_LEVELS), jax.random.fold_in(key_list[2], 1), 0, DEPTH_LEVELS - 1).astype(jnp.int32),
        "timestep": place_ends(jax.random.randint(key_list[3], (IMAGE_BATCH,), 0, STEPS_T), jax.random.fold_in(key_list[3], 1), 0, STEPS_T - 1).astype(jnp.int32),
        "segment_label_embedding": bell_draw(key_list[4], (SEG_CLASSES, MODEL_WIDTH), 0.5, 3.0),
        "depth_level_embedding": bell_draw(key_list[5], (DEPTH_LEVELS, MODEL_WIDTH), 0.5, 3.0),
        "timestep_weight": bell_draw(key_list[6], (FREQS, MODEL_WIDTH), 0.15, 0.875),
        "control_norm_gain": jnp.clip(1.0 + 0.18 * jax.random.normal(key_list[7], (MODEL_WIDTH,), jnp.float32), 0.1, 1.9),
        "control_output_weight": bell_draw(key_list[8], (MODEL_WIDTH, MODEL_WIDTH), MODEL_WIDTH ** -0.5, 0.109375, ((0, 8),)),
        "transformer_hidden_state": bell_draw(key_list[9], (IMAGE_BATCH, PATCH_ROWS, PATCH_COLUMNS, MODEL_WIDTH), 0.5, 3.0, ((0, 8), (1, 16))),
        "query": draw_query(jax.random.fold_in(key_list[14], 71), 0),
        "key": draw_key(jax.random.fold_in(key_list[14], 71), 0),
        "value": bell_draw(key_list[12], (IMAGE_BATCH, PATCH_ROWS, PATCH_COLUMNS, INNER), 2.0, 12.0, ((0, 8), (1, 16))),
        "attention_output_weight": bell_draw(key_list[13], (INNER, MODEL_WIDTH), INNER ** -0.5, 0.125, ((0, 8),)),
    }


def time_embed(timestep, timestep_weight):
    half = FREQS // 2
    freqs = jnp.exp(-math.log(10000.0) * jnp.arange(half, dtype=jnp.float32) / half)
    angles = timestep.astype(jnp.float32)[:, None] * freqs[None, :]
    features = jnp.concatenate([jnp.cos(angles), jnp.sin(angles)], axis=1).astype(jnp.bfloat16)
    return jax.nn.silu(jnp.dot(features, timestep_weight, preferred_element_type=jnp.float32))

def attend_head(entry_list):
    query_rows, input_keys, value_rows = entry_list
    scores = jnp.dot(query_rows, input_keys.T, preferred_element_type=jnp.float32) * HEAD_DIM ** (-0.5)
    peak = lax.optimization_barrier(jnp.max(scores, axis=1, keepdims=True))
    weights = jnp.exp(scores - peak)
    totals = lax.optimization_barrier(jnp.sum(weights, axis=1, keepdims=True))
    mixed = jnp.dot(weights.astype(jnp.bfloat16), value_rows, preferred_element_type=jnp.float32) / totals
    return mixed.astype(jnp.bfloat16)

def per_head(array):
    return jnp.transpose(array.reshape(TOKENS, HEADS, HEAD_DIM), (1, 0, 2))

def reference(control_hidden_state, patch_segment_labels, patch_depth_levels, timestep, segment_label_embedding, depth_level_embedding, timestep_weight, control_norm_gain, control_output_weight, transformer_hidden_state, query, key, value, attention_output_weight):
    timestep_gain = time_embed(timestep, timestep_weight)

    def single_image(entry_list):
        hidden_state, segment_vectors, depth_vectors, gain_vector, transformer_rows, query_rows, input_keys, value_rows = entry_list
        mixed = hidden_state.reshape(-1, MODEL_WIDTH).astype(jnp.float32) + segment_label_embedding[segment_vectors.reshape(-1)].astype(jnp.float32) + depth_level_embedding[depth_vectors.reshape(-1)].astype(jnp.float32)
        scale = lax.rsqrt(lax.optimization_barrier(jnp.mean(mixed * mixed, axis=-1, keepdims=True)) + 1e-06)
        normed = (mixed * scale * control_norm_gain * (1.0 + gain_vector)).astype(jnp.bfloat16)
        control_residual = jnp.dot(normed, control_output_weight, preferred_element_type=jnp.float32).astype(jnp.bfloat16)
        attended = lax.map(attend_head, (per_head(query_rows), per_head(input_keys), per_head(value_rows)))
        joined = jnp.transpose(attended, (1, 0, 2)).reshape(TOKENS, HEADS * HEAD_DIM)
        projected_rows = jnp.dot(joined, attention_output_weight, preferred_element_type=jnp.float32)
        final_output = transformer_rows.reshape(-1, MODEL_WIDTH).astype(jnp.float32) + gain_vector * projected_rows + control_residual.astype(jnp.float32)
        return final_output.astype(jnp.bfloat16).reshape(PATCH_ROWS, PATCH_COLUMNS, MODEL_WIDTH)
    return lax.map(single_image, (control_hidden_state, patch_segment_labels, patch_depth_levels, timestep_gain, transformer_hidden_state, query, key, value))
```

```python
import math

import jax
import jax.numpy as jnp
from jax import lax
from jax.experimental import pallas as pl
from jax.experimental.pallas import tpu as pltpu
from jax.sharding import PartitionSpec as P

HEADS = 16
HEAD_DIM = 128
AXES = ("ctl", "seq")
VMEM = pltpu.CompilerParams(vmem_limit_bytes=60 * 1024 * 1024)
ANY = pl.BlockSpec(memory_space=pl.ANY)
SMEM = pl.BlockSpec(memory_space=pltpu.SMEM)
FULL = pl.BlockSpec(memory_space=pltpu.VMEM)


def _coords(ctl, seq):
    z, y_hi = ctl // 2, ctl % 2
    y_lo, x, core = seq // 8, (seq // 2) % 4, seq % 2
    return x, y_hi * 2 + y_lo, z, core


def _device(x, y, z, core):
    x, y, z = x % 4, y % 4, z % 4
    return (z * 2 + y // 2) * 16 + (y % 2) * 8 + x * 2 + core


def _route(move):
    return [(d, _device(*move(*_coords(d // 16, d % 16)))) for d in range(128)]


Z_UP = _route(lambda x, y, z, k: (x, y, z + 1, k))
Z_DOWN = _route(lambda x, y, z, k: (x, y, z - 1, k))
Y_OTHER = _route(lambda x, y, z, k: (x, 3 - y, z, k))
CORE = _route(lambda x, y, z, k: (x, y, z, 1 - k))


def send(value, route):
    return lax.ppermute(value, AXES, route)


def time_embed(timestep, timestep_weight):
    half = timestep_weight.shape[0] // 2
    freqs = jnp.exp(-math.log(10000.0) * jnp.arange(half, dtype=jnp.float32) / half)
    angles = timestep.astype(jnp.float32)[:, None] * freqs[None, :]
    features = jnp.concatenate([jnp.cos(angles), jnp.sin(angles)], axis=1).astype(jnp.bfloat16)
    return jax.nn.silu(jnp.dot(features, timestep_weight, preferred_element_type=jnp.float32))


def _normed_body(src, seg_idx, dep_idx, hidden, seg, dep, gain, out, table, sem, cond):
    tokens = src.shape[0]
    width = hidden.shape[1]
    classes = seg.shape[0]
    levels = dep.shape[0]
    copies = [
        pltpu.make_async_copy(hidden, table.at[pl.ds(0, tokens)], sem.at[0]),
        pltpu.make_async_copy(dep, table.at[pl.ds(tokens, levels)], sem.at[1]),
    ]
    for c in copies:
        c.start()
    base = tokens + levels
    table[pl.ds(base + 128, 128)] = jnp.zeros((128, width), jnp.bfloat16)
    table[pl.ds(base, classes)] = seg[...]
    iota = lambda n: lax.broadcasted_iota(jnp.int32, (tokens, n), 1)
    pick = jnp.concatenate(
        [
            (iota(tokens) == src[...]).astype(jnp.bfloat16),
            (iota(levels) == dep_idx[...]).astype(jnp.bfloat16),
            (iota(256) == seg_idx[...]).astype(jnp.bfloat16),
        ],
        axis=1,
    )
    for c in copies:
        c.wait()
    step = 512
    square = jnp.zeros((tokens, 1), jnp.float32)
    for n in range(width // step):
        mixed = jnp.dot(pick, table[:, n * step : (n + 1) * step], preferred_element_type=jnp.float32)
        cond[:, n * step : (n + 1) * step] = mixed
        square = square + jnp.sum(mixed * mixed, axis=1, keepdims=True)
    scale = lax.rsqrt(square * (1.0 / width) + 1e-06)
    for n in range(width // step):
        part = slice(n * step, (n + 1) * step)
        out[:, part] = (cond[:, part] * scale * gain[:, part]).astype(jnp.bfloat16)


def normed_features(hidden, seg_idx, dep_idx, seg, dep, gain):
    _, rows, cols, width = hidden.shape
    tokens = rows * cols
    by_column = jnp.transpose(hidden, (0, 2, 1, 3)).reshape(tokens, width)
    t = jnp.arange(tokens, dtype=jnp.int32)
    src = ((t % cols) * rows + t // cols).reshape(tokens, 1)
    return pl.pallas_call(
        _normed_body,
        out_shape=jax.ShapeDtypeStruct((tokens, width), jnp.bfloat16),
        in_specs=[FULL, FULL, FULL, ANY, FULL, ANY, FULL],
        out_specs=FULL,
        scratch_shapes=[
            pltpu.VMEM((tokens + dep.shape[0] + 256, width), jnp.bfloat16),
            pltpu.SemaphoreType.DMA((2,)),
            pltpu.VMEM((tokens, width), jnp.float32),
        ],
        compiler_params=VMEM,
        name="normed",
    )(src, seg_idx.reshape(tokens, 1), dep_idx.reshape(tokens, 1), by_column, seg, dep, gain)


def _pack_body(query, keys, values, out, sem):
    heads = out.shape[0]
    copies = []
    for h in range(heads):
        for i, rows in enumerate((query, keys, values)):
            copies.append(
                pltpu.make_async_copy(
                    rows.at[:, pl.ds(h * HEAD_DIM, HEAD_DIM)], out.at[h, i], sem.at[h * 3 + i]
                )
            )
    for c in copies:
        c.start()
    for c in copies:
        c.wait()


def pack(query, keys, values):
    rows = query.shape[0]
    return pl.pallas_call(
        _pack_body,
        out_shape=jax.ShapeDtypeStruct((HEADS, 3, rows, HEAD_DIM), jnp.bfloat16),
        in_specs=[ANY] * 3,
        out_specs=ANY,
        scratch_shapes=[pltpu.SemaphoreType.DMA((HEADS * 3,))],
        compiler_params=VMEM,
        name="pack",
    )(query, keys, values)


def _attend_body(packed, out, keys, values, scores, sem):
    blocks, _, rows, _ = packed.shape
    length = blocks * rows
    scale = HEAD_DIM ** (-0.5) * math.log2(math.e)
    keys[...] = packed[:, 1].reshape(length, HEAD_DIM)
    values[:, 0:HEAD_DIM] = packed[:, 2].reshape(length, HEAD_DIM)
    values[:, HEAD_DIM:] = jnp.ones((length, HEAD_DIM), jnp.bfloat16)

    def score(index):
        return lax.dot_general(
            packed[index, 0], keys[...], (((1,), (1,)), ((), ())), preferred_element_type=jnp.float32
        )

    scores[0] = score(0)

    def step(index, _):
        current = scores[index % 2]
        peak = jnp.max(current, axis=1, keepdims=True)
        weights = jnp.exp2((current - peak) * scale).astype(jnp.bfloat16)
        scores[(index + 1) % 2] = score(jnp.minimum(index + 1, blocks - 1))
        mixed = jnp.dot(weights, values[...], preferred_element_type=jnp.float32)
        out[index] = (mixed[:, 0:HEAD_DIM] / mixed[:, HEAD_DIM : HEAD_DIM + 1]).astype(jnp.bfloat16)
        return 0

    lax.fori_loop(0, blocks, step, 0)


def attend(packed):
    blocks, _, rows, _ = packed.shape
    length = blocks * rows
    return pl.pallas_call(
        _attend_body,
        out_shape=jax.ShapeDtypeStruct((blocks, rows, HEAD_DIM), jnp.bfloat16),
        in_specs=[FULL],
        out_specs=FULL,
        scratch_shapes=[
            pltpu.VMEM((length, HEAD_DIM), jnp.bfloat16),
            pltpu.VMEM((length, 2 * HEAD_DIM), jnp.bfloat16),
            pltpu.VMEM((2, rows, length), jnp.float32),
            pltpu.SemaphoreType.DMA((3,)),
        ],
        compiler_params=VMEM,
        name="attend",
    )(packed)


def _weight_copies(pieces, weights, yh, sems):
    rows = weights.shape[2]
    half = rows // 2
    own, oth = [], []
    copies = []
    for pair in range(4):
        group = []
        for which in range(2):
            piece = pieces[pair][which]
            slot = yh if which == 0 else 1 - yh
            if isinstance(piece, tuple):
                group.append(pltpu.make_async_copy(piece[0], weights.at[pair, slot, pl.ds(0, half)], sems.at[pair * 3]))
                group.append(pltpu.make_async_copy(piece[1], weights.at[pair, slot, pl.ds(half, half)], sems.at[pair * 3 + 1]))
            else:
                group.append(pltpu.make_async_copy(piece, weights.at[pair, slot], sems.at[pair * 3 + which * 2]))
        copies.append(group)
    return copies


def _multiply(rows_ref, weights, acc, copies):
    cols = acc.shape[1]
    step = 512
    for pair in range(4):
        for c in copies[pair]:
            c.wait()
        for n in range(cols // step):
            part = slice(n * step, (n + 1) * step)
            block = weights[pair, :, :, part].reshape(-1, step)
            product = jnp.dot(rows_ref[pair], block, preferred_element_type=jnp.float32)
            if pair == 0:
                acc[:, part] = product
            else:
                acc[:, part] += product


def _control_body(place, order, mine, other, w0, w1, w2, w3, w4, w5, w6a, w6b, w7, out_mine, out_other, rows, weights, acc, sem_w, sem_r):
    pieces = ((w0, w1), (w2, w3), (w4, w5), ((w6a, w6b), w7))
    tokens = mine.shape[0]
    width = rows.shape[2]
    copies = _weight_copies(pieces, weights, place[4], sem_w)
    for pair in range(4):
        for i, source in enumerate((mine, other)):
            at = pl.multiple_of(place[pair] * width, width)
            copies[pair].append(
                pltpu.make_async_copy(
                    source.at[:, pl.ds(at, width)], rows.at[pair, pl.ds(i * tokens, tokens)], sem_r.at[pair * 2 + i]
                )
            )
    for group in copies:
        for c in group:
            c.start()
    _multiply(rows, weights, acc, copies)
    pick = (lax.broadcasted_iota(jnp.int32, (tokens, tokens), 1) == order[...]).astype(jnp.bfloat16)
    for i, out in enumerate((out_mine, out_other)):
        for n in range(acc.shape[1] // 512):
            part = slice(n * 512, (n + 1) * 512)
            residual = acc[pl.ds(i * tokens, tokens), part].astype(jnp.bfloat16)
            out[:, part] = jnp.dot(pick, residual, preferred_element_type=jnp.float32).astype(jnp.bfloat16)


def control_project(place, order, mine, other, pieces):
    tokens = mine.shape[0]
    rows, cols = pieces[0].shape
    shape = jax.ShapeDtypeStruct((tokens, cols), jnp.bfloat16)
    return pl.pallas_call(
        _control_body,
        out_shape=(shape, shape),
        in_specs=[SMEM, FULL] + [ANY] * 11,
        out_specs=(FULL, FULL),
        scratch_shapes=[
            pltpu.VMEM((4, 2 * tokens, 2 * rows), jnp.bfloat16),
            pltpu.VMEM((4, 2, rows, cols), jnp.bfloat16),
            pltpu.VMEM((2 * tokens, cols), jnp.float32),
            pltpu.SemaphoreType.DMA((12,)),
            pltpu.SemaphoreType.DMA((8,)),
        ],
        compiler_params=VMEM,
        name="control_project",
    )(place, order, mine, other, *pieces)


def _output_body(place, gain, m0, m1, o0, o1, res_mine, res_other, w0, w1, w2, w3, w4, w5, w6a, w6b, w7, out_mine, out_other, rows, weights, acc, sem_w, sem_r):
    pieces = ((w0, w1), (w2, w3), (w4, w5), ((w6a, w6b), w7))
    tokens = m0.shape[1]
    per_pair = rows.shape[2] // HEAD_DIM
    copies = _weight_copies(pieces, weights, place[4], sem_w)
    for pair in range(4):
        for i, source in enumerate((m0, m1, o0, o1)):
            for h in range(per_pair):
                copies[pair].append(
                    pltpu.make_async_copy(
                        source.at[place[pair] * per_pair + h],
                        rows.at[pair, pl.ds(i * tokens, tokens), pl.ds(h * HEAD_DIM, HEAD_DIM)],
                        sem_r.at[(pair * 4 + i) * per_pair + h],
                    )
                )
    for group in copies:
        for c in group:
            c.start()
    _multiply(rows, weights, acc, copies)
    for i, (out, res) in enumerate(((out_mine, res_mine), (out_other, res_other))):
        for image in range(2):
            at = pl.ds(image * tokens, tokens)
            projected = acc[pl.ds((i * 2 + image) * tokens, tokens)]
            out[at] = (gain[image : image + 1] * projected + res[at].astype(jnp.float32)).astype(jnp.bfloat16)


def output_project(place, gain, attended, residual, pieces):
    tokens = attended[0].shape[1]
    rows, cols = pieces[0].shape
    shape = jax.ShapeDtypeStruct((2 * tokens, cols), jnp.bfloat16)
    per_pair = 2 * rows // HEAD_DIM
    return pl.pallas_call(
        _output_body,
        out_shape=(shape, shape),
        in_specs=[SMEM, FULL] + [ANY] * 4 + [FULL] * 2 + [ANY] * 9,
        out_specs=(FULL, FULL),
        scratch_shapes=[
            pltpu.VMEM((4, 4 * tokens, 2 * rows), jnp.bfloat16),
            pltpu.VMEM((4, 2, rows, cols), jnp.bfloat16),
            pltpu.VMEM((4 * tokens, cols), jnp.float32),
            pltpu.SemaphoreType.DMA((12,)),
            pltpu.SemaphoreType.DMA((16 * per_pair,)),
        ],
        compiler_params=VMEM,
        name="output_project",
    )(place, gain, *attended, *residual, *pieces)


def gather_first(own):
    return send(own, Z_UP), send(own, Z_DOWN), send(own, Y_OTHER)


def gather_second(first):
    below, above, across = first
    half = below.shape[0] // 2
    return (
        send(above, Y_OTHER),
        send(across, Z_UP),
        send(below[:half], Z_UP),
        send(above[half:], Z_DOWN),
    )


def gather_third(second):
    return send(second[0], Z_DOWN)


def in_pairs(own, first, second, third):
    below, above, across = first
    above_across, below_across, far_a, far_b = second
    return (own, across, below, below_across, above, above_across, far_a, far_b, third)


def per_device(
    control_hidden_state,
    patch_segment_labels,
    patch_depth_levels,
    timestep,
    segment_label_embedding,
    depth_level_embedding,
    timestep_weight,
    control_norm_gain,
    control_output_weight,
    transformer_hidden_state,
    query,
    key,
    value,
    attention_output_weight,
):
    ctl = lax.axis_index("ctl")
    seq = lax.axis_index("seq")
    core = seq % 2
    z = ctl // 2
    width = control_hidden_state.shape[-1]
    half = width // 2
    images, patch_rows, columns, _ = transformer_hidden_state.shape
    tokens = patch_rows * columns
    seqs = HEADS
    ctls = 8
    place = jnp.stack([z, (z + 3) % 4, (z + 1) % 4, (z + 2) % 4, ctl % 2]).astype(jnp.int32)

    mine_c = lax.dynamic_slice_in_dim(control_output_weight, core * half, half, 1)
    mine_o = lax.dynamic_slice_in_dim(attention_output_weight, core * half, half, 1)
    first_c = gather_first(mine_c)
    first_o = gather_first(mine_o)

    flat = lambda a, i: a[i].reshape(tokens, a.shape[-1])
    swap = lambda a, axis: lax.all_to_all(a, axis, split_axis=0, concat_axis=0, tiled=True)
    packed = [swap(pack(flat(query, i), flat(key, i), flat(value, i)), "seq") for i in range(images)]

    timestep_gain = time_embed(timestep, timestep_weight)
    control_gain = control_norm_gain[None, :] * (1.0 + lax.dynamic_slice_in_dim(timestep_gain, seq, 1, 0))
    normed = normed_features(
        control_hidden_state,
        patch_segment_labels,
        patch_depth_levels,
        segment_label_embedding,
        depth_level_embedding,
        control_gain,
    )
    part = normed.shape[0] // seqs
    moved = swap(normed.reshape(seqs, part, width), "seq")
    moved = swap(moved.reshape(ctls, seqs // ctls, part, width), "ctl").reshape(-1, width)
    moved_other = send(moved, CORE)

    second_c = gather_second(first_c)
    second_o = gather_second(first_o)
    third_c = gather_third(second_c)
    third_o = gather_third(second_o)

    attended = [swap(attend(p), "seq") for p in packed]
    attended_other = [send(a, CORE) for a in attended]

    per_ctl = columns // ctls
    t = jnp.arange(images * tokens, dtype=jnp.int32)
    image, row, col = t // tokens, (t // columns) % patch_rows, t % columns
    order = (((col // per_ctl) * images + image) * part + row * per_ctl + col % per_ctl).reshape(-1, 1)
    residual = control_project(place, order, moved, moved_other, in_pairs(mine_c, first_c, second_c, third_c))

    gain = lax.dynamic_slice(timestep_gain, (ctl * images, core * half), (images, half))
    done_mine, done_other = output_project(
        place, gain, attended + attended_other, residual, in_pairs(mine_o, first_o, second_o, third_o)
    )
    done_received = send(done_other, CORE)
    low = jnp.where(core == 0, done_mine, done_received)
    high = jnp.where(core == 0, done_received, done_mine)
    update = jnp.concatenate([low, high], axis=1).astype(jnp.float32)
    result = transformer_hidden_state.reshape(-1, width).astype(jnp.float32) + update
    return result.astype(jnp.bfloat16).reshape(transformer_hidden_state.shape)


def solution(mesh):
    return jax.shard_map(
        per_device,
        mesh=mesh,
        in_specs=(
            P("seq", None, "ctl", None),
            P("seq", None, "ctl"),
            P("seq", None, "ctl"),
            P(),
            P(),
            P(),
            P(),
            P(),
            P("ctl", None),
            P("ctl", "seq", None, None),
            P("ctl", "seq", None, None),
            P("ctl", "seq", None, None),
            P("ctl", "seq", None, None),
            P("ctl", None),
        ),
        out_specs=P("ctl", "seq", None, None),
        check_vma=False,
    )
```
